32 devices in a mesh: parts: 2 (over x), tok: 8 (over z, y), sub: 2 (over core).
Axes of the slice: x: 2, y: 2, z: 4, core: 2. Of those that a mesh axis runs over, the one named last changes fastest.
Arguments:
- video: bfloat16 [16, 48, 16, 768], P('parts', None, ('tok', 'sub')), parts along dimension 0, may hold values from -6 to 6
- norm_gain: float32 [3, 768], replicated, may hold values from 0.1 to 1.9
- qkv_weight: bfloat16 [3, 3, 768, 768], P(None, None, None, 'sub'), may hold values from -0.21875 to 0.21875
- out_weight: bfloat16 [3, 768, 768], P(None, 'sub'), may hold values from -0.21875 to 0.21875
Outputs:
- refined: bfloat16 [16, 48, 16, 768], P('parts', None, ('tok', 'sub')), parts along dimension 0
The draws below stay inside these ranges and needn't reach their ends.
There are 2 independent parts, one for each index of `parts`. The reference program is written for one: setup_inputs(seed, part) draws one part's arguments, and reference() takes and returns one part's arrays. A program takes and returns all parts, laid end to end along the dimension named above; an argument that names none is the same for every part. Nothing has to cross between parts.
All inputs are finite; a program needn't handle non-finite values.
Results may differ from the reference program's by a relative error of at most 0.014.
Values may be sent and summed in bfloat16 or wider, within the bound.
No kernel may reach another device: no remote copies, remote signals or barrier semaphores. Data moves between devices by JAX's collectives and lax.ppermute only.
A program may use at most 64 MiB of HBM per device.

```python
import math
import jax
import jax.numpy as jnp
from jax import lax

D = 768
HEAD_DIM = 64
T_SIZE = 8
H = 48
W = 16


def levels(rng, extent, shards, least, high):
    loudness, own = 1.0, jax.random.fold_in(rng, 6)
    for position, parts in shards:
        draws = jnp.exp(jax.random.uniform(jax.random.fold_in(own, position), (parts,), jnp.float32, least / len(shards), high / len(shards)))
        loudness = loudness * jnp.repeat(draws, extent[position] // parts).reshape([-1 if axis == position else 1 for axis in range(len(extent))])
    return loudness


def normal_values(key, extent, scale, reach, shards=(), held_as=jnp.bfloat16):
    loudness = levels(key, extent, shards, -0.22, 0.18) if shards else 1.0
    result = jax.random.normal(key, extent, jnp.float32) * scale * loudness
    return jnp.minimum(jnp.maximum(result, -reach), reach).astype(held_as)


def setup_inputs(seed: int = 0, part: int = 0) -> dict:
    splits = jax.random.split(jax.random.key(seed), 5)
    part_keys = jax.random.split(jax.random.fold_in(splits[4], part), 5)
    return {
        "video": normal_values(part_keys[0], (T_SIZE, H, W, D), 1.0, 6.0, ((2, 16),)),
        "norm_gain": jnp.clip(1.0 + 0.18 * jax.random.normal(splits[1], (3, D), jnp.float32), 0.1, 1.9),
        "qkv_weight": normal_values(splits[2], (3, 3, D, D), D ** -0.5, 0.21875, ((3, 2),)),
        "out_weight": normal_values(splits[3], (3, D, D), D ** -0.5, 0.21875, ((1, 2),)),
    }


EPSILON = 1e-06

def normalize(tokens, gain):
    values = tokens.astype(jnp.float32)
    scale = lax.rsqrt(lax.optimization_barrier(jnp.mean(values * values, axis=-1, keepdims=True)) + EPSILON)
    return (values * scale * gain.astype(jnp.float32)).astype(jnp.bfloat16)

def head_norm(values, shape):
    split = values.reshape(shape + (values.shape[-1] // HEAD_DIM, HEAD_DIM))
    scale = lax.rsqrt(lax.optimization_barrier(jnp.mean(split * split, axis=-1, keepdims=True)) + EPSILON)
    return (split * scale).astype(jnp.bfloat16)

def attend(query, key, value, shape):
    query_n = head_norm(query, shape)
    key_n = head_norm(key, shape)
    value_b = value.reshape(query_n.shape).astype(jnp.bfloat16)
    scores = jnp.einsum('plqhe,pmqhe->pqhlm', query_n.astype(jnp.float32), key_n.astype(jnp.float32)) / math.sqrt(HEAD_DIM)
    expo = jnp.exp(scores)
    probs = (expo / lax.optimization_barrier(jnp.sum(expo, axis=-1, keepdims=True))).astype(jnp.bfloat16)
    mixed = jnp.einsum('pqhlm,pmqhe->plqhe', probs.astype(jnp.float32), value_b.astype(jnp.float32))
    return mixed.astype(jnp.bfloat16).reshape(query.shape)

def sublayer(tokens, gain, qkv_part, out_part):
    shape = tokens.shape[:3]
    width = tokens.shape[3]
    flat = normalize(tokens, gain).reshape(-1, width)
    query = jnp.dot(flat, qkv_part[0], preferred_element_type=jnp.float32)
    key = jnp.dot(flat, qkv_part[1], preferred_element_type=jnp.float32)
    value = jnp.dot(flat, qkv_part[2], preferred_element_type=jnp.float32)
    mixed = attend(query, key, value, shape)
    update = jnp.dot(mixed, out_part, preferred_element_type=jnp.float32).reshape(tokens.shape)
    return (tokens.astype(jnp.float32) + update).astype(jnp.bfloat16)

def reference(video, norm_gain, qkv_weight, out_weight):
    frames, rows, cols, width = video.shape
    state = sublayer(video.reshape(1, frames, rows * cols, width), norm_gain[0], qkv_weight[0], out_weight[0]).reshape(video.shape)

    def across(frame):
        return sublayer(frame.reshape(rows, cols, 1, width), norm_gain[1], qkv_weight[1], out_weight[1]).reshape(frame.shape)
    state = lax.map(across, state)

    def downward(frame):
        return sublayer(frame.reshape(1, rows, cols, width), norm_gain[2], qkv_weight[2], out_weight[2]).reshape(frame.shape)
    return lax.map(downward, state)
```

```python
import functools
import math

import jax
import jax.numpy as jnp
from jax import lax
from jax.experimental import pallas as pl
from jax.experimental.pallas import tpu as pltpu
from jax.sharding import PartitionSpec as P

HEAD_DIM = 64
LANES = 128
EPSILON = 1e-06

VMEM = pl.BlockSpec(memory_space=pltpu.VMEM)
ANY = pl.BlockSpec(memory_space=pl.ANY)


def selection(source, count):
    column = lax.broadcasted_iota(jnp.int32, (source.shape[0], count), 1)
    return jnp.where(source == column, 1.0, 0.0).astype(jnp.bfloat16)


def row_index(count):
    return lax.broadcasted_iota(jnp.int32, (count, 1), 0)


def pick(matrix, values):
    return jnp.dot(matrix, values, preferred_element_type=jnp.float32).astype(jnp.bfloat16)


def sublayer_body(plan, refs):
    layer, n_in, n_out = plan["layer"], plan["n_in"], len(plan["outs"])
    x_refs, refs = refs[:n_in], refs[n_in:]
    gain_ref, qkv_own, qkv_far, out_own, out_far = refs[:5]
    o_refs, refs = refs[5 : 5 + n_out], refs[5 + n_out :]
    w_ref, wo_ref, q_ref, k_ref, v_ref, m_ref, sems = refs
    half = qkv_own.shape[-1]
    width = 2 * half
    copies = []
    for j in range(3):
        for side, source in enumerate((qkv_own, qkv_far)):
            copies.append(
                pltpu.make_async_copy(
                    source.at[layer, j],
                    w_ref.at[j, :, pl.ds(side * half, half)],
                    sems.at[2 * j + side],
                )
            )
    for side, source in enumerate((out_own, out_far)):
        copies.append(
            pltpu.make_async_copy(
                source.at[layer], wo_ref.at[pl.ds(side * half, half), :], sems.at[6 + side]
            )
        )
    for copy in copies:
        copy.start()

    x = jnp.concatenate([r[...] for r in x_refs], axis=0) if n_in > 1 else x_refs[0][...]
    count = x.shape[0]
    if plan["enter"] is not None:
        x = pick(selection(plan["enter"](), count), x)
    values = x.astype(jnp.float32)
    scale = lax.rsqrt(jnp.mean(values * values, axis=-1, keepdims=True) + EPSILON)
    normed = (values * scale * gain_ref[pl.ds(layer, 1), :]).astype(jnp.bfloat16)
    if plan["inner"] is not None:
        normed = pick(selection(plan["inner"](), count), normed)

    wide = 4 * HEAD_DIM
    if width % wide:
        wide = LANES
    a = lax.broadcasted_iota(jnp.int32, (wide, wide), 0) // HEAD_DIM
    b = lax.broadcasted_iota(jnp.int32, (wide, wide), 1) // HEAD_DIM
    average = jnp.where(a == b, 1.0 / HEAD_DIM, 0.0).astype(jnp.bfloat16)
    for j, (ref, factor) in enumerate(
        ((q_ref, math.log2(math.e) / math.sqrt(HEAD_DIM)), (k_ref, 1.0), (v_ref, None))
    ):
        copies[2 * j].wait()
        copies[2 * j + 1].wait()
        y = jnp.dot(normed, w_ref[j], preferred_element_type=jnp.float32)
        if factor is None:
            ref[...] = y.astype(jnp.bfloat16)
            continue
        squares = (y * y).astype(jnp.bfloat16)
        for at in range(0, width, wide):
            mean = jnp.dot(
                squares[:, at : at + wide], average, preferred_element_type=jnp.float32
            )
            ref[:, at : at + wide] = (
                y[:, at : at + wide] * (lax.rsqrt(mean + EPSILON) * factor)
            ).astype(jnp.bfloat16)

    block = plan["block"]
    lane = lax.broadcasted_iota(jnp.int32, (1, LANES), 1)
    first = jnp.where(lane < HEAD_DIM, 1.0, 0.0).astype(jnp.bfloat16)
    second = jnp.where(lane < HEAD_DIM, 0.0, 1.0).astype(jnp.bfloat16)
    row = lax.broadcasted_iota(jnp.int32, (block, 2 * block), 0)
    col = lax.broadcasted_iota(jnp.int32, (block, 2 * block), 1)
    keep = plan["mask"](row, jnp.where(col >= block, col - block, col))
    ones = jnp.concatenate(
        [jnp.broadcast_to(first, (block, LANES)), jnp.broadcast_to(second, (block, LANES))], 0
    )

    def pair(p, carry):
        lanes = pl.ds(pl.multiple_of(p * LANES, LANES), LANES)
        for at in range(0, count, block):
            rows = pl.ds(at, block)
            q, k, v = q_ref[rows, lanes], k_ref[rows, lanes], v_ref[rows, lanes]
            keys = jnp.concatenate([k * first, k * second], 0)
            score = lax.dot_general(
                q, keys, (((1,), (1,)), ((), ())), preferred_element_type=jnp.float32
            )
            expo = jnp.where(keep, jnp.exp2(score), 0.0).astype(jnp.bfloat16)
            vals = jnp.concatenate(
                [jnp.concatenate([v * first, v * second], 0), ones], 1
            )
            both = jnp.dot(expo, vals, preferred_element_type=jnp.float32)
            m_ref[rows, lanes] = (both[:, :LANES] / both[:, LANES:]).astype(jnp.bfloat16)
        return carry

    lax.fori_loop(0, width // LANES, pair, 0)
    mixed = m_ref[...]
    if plan["leave"] is not None:
        mixed = pick(selection(plan["leave"](), count), mixed)
    copies[6].wait()
    copies[7].wait()
    update = jnp.dot(mixed, wo_ref[...], preferred_element_type=jnp.float32)
    result = (x.astype(jnp.float32) + update).astype(jnp.bfloat16)
    for ref, pieces in zip(o_refs, plan["outs"]):
        at = 0
        for start, size in pieces:
            ref[pl.ds(at, size), :] = result[start : start + size]
            at += size


def sublayer(xs, weights, layer, block, mask, outs, enter=None, inner=None, leave=None, name="sublayer"):
    count = sum(x.shape[0] for x in xs)
    width = xs[0].shape[1]
    plan = dict(
        layer=layer, n_in=len(xs), outs=outs, block=block, mask=mask,
        enter=enter, inner=inner, leave=leave,
    )

    def kernel(*refs):
        sublayer_body(plan, refs)

    flops = 2 * count * width * width * 5
    return pl.pallas_call(
        kernel,
        out_shape=[
            jax.ShapeDtypeStruct((sum(size for _, size in pieces), width), jnp.bfloat16)
            for pieces in outs
        ],
        in_specs=[VMEM] * (len(xs) + 1) + [ANY] * 4,
        out_specs=[VMEM] * len(outs),
        scratch_shapes=[
            pltpu.VMEM((3, width, width), jnp.bfloat16),
            pltpu.VMEM((width, width), jnp.bfloat16),
        ]
        + [pltpu.VMEM((count, width), jnp.bfloat16)] * 4
        + [pltpu.SemaphoreType.DMA((8,))],
        compiler_params=pltpu.CompilerParams(vmem_limit_bytes=40 << 20),
        cost_estimate=pl.CostEstimate(
            flops=flops, bytes_accessed=8 * width * width + 4 * count * width, transcendentals=0
        ),
        name=name,
    )(*xs, *weights)


def gather_weights(norm_gain, qkv_weight, out_weight):
    swap = [(0, 1), (1, 0)]
    return (
        norm_gain,
        qkv_weight,
        lax.ppermute(qkv_weight, "sub", swap),
        out_weight,
        lax.ppermute(out_weight, "sub", swap),
    )


def general(video, weights):
    frames, rows, cols, width = video.shape
    count = frames * rows * cols
    devices = lax.axis_size("tok") * lax.axis_size("sub")
    lines = frames * rows // devices
    wide = devices * cols

    def whole(n):
        return [[(0, n)]]

    def divisor(line):
        best = line
        for groups in range(1, count // line + 1):
            size = groups * line
            if count % size == 0 and size % 16 == 0 and (size <= LANES or best % 16):
                best = size
        return best

    def by_place():
        at = row_index(count)
        return lax.rem(at, frames) * (rows * cols) + lax.div(at, frames)

    def by_frame():
        at = row_index(count)
        return lax.rem(at, rows * cols) * frames + lax.div(at, rows * cols)

    def same(line):
        return lambda i, j: lax.div(i, line) == lax.div(j, line)

    (state,) = sublayer(
        [video.reshape(count, width)], weights, 0, divisor(frames), same(frames), whole(count),
        inner=by_place, leave=by_frame, name="temporal",
    )
    items = lax.all_to_all(
        state.reshape(lines, devices, cols, width), ("tok", "sub"), split_axis=1, concat_axis=2, tiled=True
    )
    (turned,) = sublayer(
        [items.reshape(count, width)], weights, 1, divisor(wide), same(wide), whole(count),
        name="horizontal",
    )
    state = lax.all_to_all(
        turned.reshape(lines, 1, wide, width), ("tok", "sub"), split_axis=2, concat_axis=1, tiled=True
    )

    def by_column():
        at = row_index(count)
        f, c, r = lax.div(at, rows * cols), lax.rem(lax.div(at, rows), cols), lax.rem(at, rows)
        return f * (rows * cols) + r * cols + c

    def by_row():
        at = row_index(count)
        f, r, c = lax.div(at, rows * cols), lax.rem(lax.div(at, cols), rows), lax.rem(at, cols)
        return f * (rows * cols) + c * rows + r

    (state,) = sublayer(
        [state.reshape(count, width)], weights, 2, divisor(rows), same(rows), whole(count),
        inner=by_column if cols > 1 else None, leave=by_row if cols > 1 else None, name="vertical",
    )
    return state.reshape(video.shape)


def body(video, norm_gain, qkv_weight, out_weight):
    weights = gather_weights(norm_gain, qkv_weight, out_weight)
    return general(video, weights)


def solution(mesh):
    in_specs = (
        P("parts", None, ("tok", "sub"), None),
        P(),
        P(None, None, None, "sub"),
        P(None, "sub", None),
    )
    out_specs = P("parts", None, ("tok", "sub"), None)
    return jax.shard_map(body, mesh=mesh, in_specs=in_specs, out_specs=out_specs, check_vma=False)
```

```python
import functools
import math

import jax
import jax.numpy as jnp
from jax import lax
from jax.experimental import pallas as pl
from jax.experimental.pallas import tpu as pltpu
from jax.sharding import PartitionSpec as P

HEAD_DIM = 64
LANES = 128
EPSILON = 1e-06

VMEM = pl.BlockSpec(memory_space=pltpu.VMEM)
HBM = pl.BlockSpec(memory_space=pltpu.HBM)


def selection(source, count):
    column = lax.broadcasted_iota(jnp.int32, (source.shape[0], count), 1)
    return jnp.where(source == column, 1.0, 0.0).astype(jnp.bfloat16)


def row_index(count):
    return lax.broadcasted_iota(jnp.int32, (count, 1), 0)


def pick(matrix, values):
    return jnp.dot(matrix, values, preferred_element_type=jnp.float32).astype(jnp.bfloat16)


def transfers(layer, sources, w_ref, wo_ref, sems):
    copies = []
    half = w_ref.shape[-1] // 2
    for j in range(3):
        for side, source in enumerate(sources[0::2]):
            part = source.at[layer, j] if len(source.shape) == 4 else source.at[j]
            copies.append(
                pltpu.make_async_copy(part, w_ref.at[j, :, pl.ds(side * half, half)], sems.at[2 * j + side])
            )
    for side, source in enumerate(sources[1::2]):
        part = source.at[layer] if len(source.shape) == 3 else source
        copies.append(
            pltpu.make_async_copy(part, wo_ref.at[pl.ds(side * half, half), :], sems.at[6 + side])
        )
    return copies


def sublayer_body(plan, refs):
    layer, outs = plan["layer"], plan["outs"]
    x_refs, refs = refs[: plan["n_in"]], refs[plan["n_in"] :]
    gain_ref, refs = refs[0], refs[1:]
    here, there = [], []
    if plan["held"]:
        (w_ref, wo_ref), refs = refs[:2], refs[2:]
    else:
        here, refs = refs[:4], refs[4:]
    if plan["ahead"]:
        there, refs = refs[:4], refs[4:]
    o_refs, refs = refs[: len(outs)], refs[len(outs) :]
    if not plan["held"]:
        (w_ref, wo_ref), refs = refs[:2], refs[2:]
    if plan["ahead"]:
        following, refs = refs[:2], refs[2:]
    q_ref, k_ref, v_ref, m_ref, refs = *refs[:4], refs[4:]
    copies, later = [], []
    if here:
        copies, refs = transfers(layer, here, w_ref, wo_ref, refs[0]), refs[1:]
    if there:
        later = transfers(layer + 1, there, *following, refs[0])
    for copy in copies + later:
        copy.start()

    x = jnp.concatenate([r[...] for r in x_refs], axis=0) if len(x_refs) > 1 else x_refs[0][...]
    if plan["enter"] is not None:
        x = pick(selection(plan["enter"](), x.shape[0]), x)
    count, width = x.shape
    values = x.astype(jnp.float32)
    scale = lax.rsqrt(jnp.mean(values * values, axis=-1, keepdims=True) + EPSILON)
    normed = (values * scale * gain_ref[pl.ds(layer, 1), :]).astype(jnp.bfloat16)
    if plan["inner"] is not None:
        normed = pick(selection(plan["inner"](), count), normed)

    wide = 4 * HEAD_DIM
    if width % wide:
        wide = LANES
    a = lax.broadcasted_iota(jnp.int32, (wide, wide), 0) // HEAD_DIM
    b = lax.broadcasted_iota(jnp.int32, (wide, wide), 1) // HEAD_DIM
    average = jnp.where(a == b, 1.0 / HEAD_DIM, 0.0).astype(jnp.bfloat16)
    for j, (ref, factor) in enumerate(
        ((q_ref, math.log2(math.e) / math.sqrt(HEAD_DIM)), (k_ref, 1.0), (v_ref, None))
    ):
        for copy in copies[2 * j : 2 * j + 2]:
            copy.wait()
        y = jnp.dot(normed, w_ref[j], preferred_element_type=jnp.float32)
        if factor is None:
            ref[...] = y.astype(jnp.bfloat16)
            continue
        squares = (y * y).astype(jnp.bfloat16)
        for at in range(0, width, wide):
            mean = jnp.dot(
                squares[:, at : at + wide], average, preferred_element_type=jnp.float32
            )
            ref[:, at : at + wide] = (
                y[:, at : at + wide] * (lax.rsqrt(mean + EPSILON) * factor)
            ).astype(jnp.bfloat16)

    block = plan["block"]
    lane = lax.broadcasted_iota(jnp.int32, (1, LANES), 1)
    first = jnp.where(lane < HEAD_DIM, 1.0, 0.0).astype(jnp.bfloat16)
    second = jnp.where(lane < HEAD_DIM, 0.0, 1.0).astype(jnp.bfloat16)
    row = lax.broadcasted_iota(jnp.int32, (block, 2 * block), 0)
    col = lax.broadcasted_iota(jnp.int32, (block, 2 * block), 1)
    keep = plan["mask"](row, jnp.where(col >= block, col - block, col))
    ones = jnp.concatenate(
        [jnp.broadcast_to(first, (block, LANES)), jnp.broadcast_to(second, (block, LANES))], 0
    )
    for p in range(0, width, LANES):
        lanes = pl.ds(p, LANES)
        for at in range(0, count, block):
            rows = pl.ds(at, block)
            q, k, v = q_ref[rows, lanes], k_ref[rows, lanes], v_ref[rows, lanes]
            keys = jnp.concatenate([k * first, k * second], 0)
            score = lax.dot_general(
                q, keys, (((1,), (1,)), ((), ())), preferred_element_type=jnp.float32
            )
            expo = jnp.where(keep, jnp.exp2(score), 0.0).astype(jnp.bfloat16)
            vals = jnp.concatenate(
                [jnp.concatenate([v * first, v * second], 0), ones], 1
            )
            both = jnp.dot(expo, vals, preferred_element_type=jnp.float32)
            m_ref[rows, lanes] = (both[:, :LANES] / both[:, LANES:]).astype(jnp.bfloat16)

    mixed = m_ref[...]
    if plan["leave"] is not None:
        mixed = pick(selection(plan["leave"](), count), mixed)
    for copy in copies[6:]:
        copy.wait()
    update = jnp.dot(mixed, wo_ref[...], preferred_element_type=jnp.float32)
    result = (x.astype(jnp.float32) + update).astype(jnp.bfloat16)
    for ref, pieces in zip(o_refs, outs):
        at = 0
        for start, size in pieces:
            ref[pl.ds(at, size), :] = result[start : start + size]
            at += size
    for copy in later:
        copy.wait()


def sublayer(
    xs, gain, layer, block, mask, outs, here=None, held=None, ahead=None, keep=False,
    enter=None, inner=None, leave=None, name="sublayer",
):
    count = sum(size for pieces in outs for _, size in pieces)
    width = xs[0].shape[1]
    plan = dict(
        layer=layer, n_in=len(xs), outs=outs, block=block, mask=mask, held=held is not None,
        ahead=ahead is not None, enter=enter, inner=inner, leave=leave,
    )

    def kernel(*refs):
        sublayer_body(plan, refs)

    both = [pltpu.VMEM((3, width, width), jnp.bfloat16), pltpu.VMEM((width, width), jnp.bfloat16)]
    out_shape = [
        jax.ShapeDtypeStruct((sum(size for _, size in pieces), width), jnp.bfloat16) for pieces in outs
    ]
    args, specs, scratch = list(xs) + [gain], [VMEM] * (len(xs) + 1), []
    if held is not None:
        args, specs = args + list(held), specs + [VMEM] * 2
    else:
        args += list(here)
        specs += [VMEM if len(w.shape) == 2 + (i % 2 == 0) else HBM for i, w in enumerate(here)]
        if keep:
            out_shape += both
        else:
            scratch += both
    if ahead is not None:
        args, specs, out_shape = args + list(ahead), specs + [HBM] * 4, out_shape + both
    scratch += [pltpu.VMEM((count, width), jnp.bfloat16)] * 4
    scratch += [pltpu.SemaphoreType.DMA((8,))] * ((held is None) + (ahead is not None))
    return pl.pallas_call(
        kernel,
        out_shape=out_shape,
        in_specs=specs,
        out_specs=[VMEM] * len(out_shape),
        scratch_shapes=scratch,
        compiler_params=pltpu.CompilerParams(vmem_limit_bytes=40 << 20),
        cost_estimate=pl.CostEstimate(
            flops=10 * count * width * width,
            bytes_accessed=8 * width * width + 4 * count * width,
            transcendentals=0,
        ),
        name=name,
    )(*args)


def gather_weights(norm_gain, qkv_weight, out_weight):
    swap = [(0, 1), (1, 0)]
    weights = (
        qkv_weight,
        out_weight,
        lax.ppermute(qkv_weight, "sub", swap),
        lax.ppermute(out_weight, "sub", swap),
    )
    return norm_gain, tuple(pltpu.with_memory_space_constraint(w, pltpu.HBM) for w in weights)


def general(video, gain, weights):
    frames, rows, cols, width = video.shape
    count = frames * rows * cols
    devices = lax.axis_size("tok") * lax.axis_size("sub")
    lines = frames * rows // devices
    wide = devices * cols

    def whole(n):
        return [[(0, n)]]

    def divisor(line):
        best = line
        for groups in range(1, count // line + 1):
            size = groups * line
            if count % size == 0 and size % 16 == 0 and (size <= LANES or best % 16):
                best = size
        return best

    def by_place():
        at = row_index(count)
        return lax.rem(at, frames) * (rows * cols) + lax.div(at, frames)

    def by_frame():
        at = row_index(count)
        return lax.rem(at, rows * cols) * frames + lax.div(at, rows * cols)

    def same(line):
        return lambda i, j: lax.div(i, line) == lax.div(j, line)

    (state,) = sublayer(
        [video.reshape(count, width)], gain, 0, divisor(frames), same(frames), whole(count), here=weights,
        inner=by_place, leave=by_frame, name="temporal",
    )
    items = lax.all_to_all(
        state.reshape(lines, devices, cols, width), ("tok", "sub"), split_axis=1, concat_axis=2, tiled=True
    )
    (turned,) = sublayer(
        [items.reshape(count, width)], gain, 1, divisor(wide), same(wide), whole(count), here=weights,
        name="horizontal",
    )
    state = lax.all_to_all(
        turned.reshape(lines, 1, wide, width), ("tok", "sub"), split_axis=2, concat_axis=1, tiled=True
    )

    def by_column():
        at = row_index(count)
        f, c, r = lax.div(at, rows * cols), lax.rem(lax.div(at, rows), cols), lax.rem(at, rows)
        return f * (rows * cols) + r * cols + c

    def by_row():
        at = row_index(count)
        f, r, c = lax.div(at, rows * cols), lax.rem(lax.div(at, cols), rows), lax.rem(at, cols)
        return f * (rows * cols) + c * rows + r

    (state,) = sublayer(
        [state.reshape(count, width)], gain, 2, divisor(rows), same(rows), whole(count), here=weights,
        inner=by_column if cols > 1 else None, leave=by_row if cols > 1 else None, name="vertical",
    )
    return state.reshape(video.shape)


def pack(x, weights, chips, piece, rows, cores):
    count, width = x.shape
    frames = count // rows
    share = piece // frames

    def kernel(x_ref, w_ref, wo_ref, *refs):
        o_refs, (w_out, wo_out, sems) = refs[:chips], refs[chips:]
        copies = [
            pltpu.make_async_copy(w_ref.at[0], w_out, sems.at[0]),
            pltpu.make_async_copy(wo_ref.at[0], wo_out, sems.at[1]),
        ]
        for copy in copies:
            copy.start()
        tok, sub = lax.axis_index("tok"), lax.axis_index("sub")
        at = row_index(count)
        k, rest = lax.div(at, cores * piece), lax.rem(at, cores * piece)
        g, t, r = lax.div(rest, piece), lax.div(lax.rem(rest, piece), share), lax.rem(rest, share)
        core = lax.rem(sub + g, cores)
        source = t * rows + ((k ^ tok) * cores + core) * share + r
        y = pick(selection(source, count), x_ref[...])
        for i, ref in enumerate(o_refs):
            ref[...] = y[i * cores * piece : (i + 1) * cores * piece]
        for copy in copies:
            copy.wait()

    return pl.pallas_call(
        kernel,
        out_shape=[jax.ShapeDtypeStruct((cores * piece, width), jnp.bfloat16)] * chips
        + [pltpu.VMEM(w.shape[1:], w.dtype) for w in weights],
        in_specs=[VMEM, HBM, HBM],
        out_specs=[VMEM] * (chips + 2),
        scratch_shapes=[pltpu.SemaphoreType.DMA((2,))],
        cost_estimate=pl.CostEstimate(
            flops=2 * count * count * width, bytes_accessed=4 * count * width, transcendentals=0
        ),
        name="pack",
    )(x, *weights)


def by_rows(video, gain, weights):
    frames, rows, _, width = video.shape
    chips, cores = lax.axis_size("tok"), lax.axis_size("sub")
    share = rows // (chips * cores)
    piece = frames * share
    count = frames * rows
    near = max(chips // 2, 1)
    groups = (range(near), range(near, chips))
    swap = [(0, 1), (1, 0)]

    def send(blocks):
        moved = list(blocks)
        for k in sorted(range(1, chips), reverse=True):
            moved[k] = lax.ppermute(blocks[k], "tok", [(i, i ^ k) for i in range(chips)])
        return moved

    *blocks, w_own, wo_own = pack(video.reshape(count, width), weights[:2], chips, piece, rows, cores)
    blocks = send(blocks)

    def within(i, j):
        return (lax.div(i, piece) == lax.div(j, piece)) & (lax.rem(i, share) == lax.rem(j, share))

    mine, theirs = [], []
    for name, group in zip(("near", "far"), groups):
        outs = [[((cores * i + g) * piece, piece) for i in range(len(group))] for g in range(cores)]
        if name == "near":
            source = dict(here=(w_own, wo_own) + weights[2:], keep=True)
        else:
            source = dict(held=held, ahead=weights)
        own, other, *held = sublayer(
            [blocks[k] for k in group], gain, 0, len(group) * cores * piece, within, outs,
            name="temporal_" + name, **source,
        )
        mine.append(own)
        theirs.append(lax.ppermute(other, "sub", swap))

    wide = chips * cores

    def to_lines():
        at = row_index(count)
        return lax.rem(at, wide) * piece + lax.div(at, wide)

    def to_pieces():
        at = row_index(count)
        return lax.rem(at, piece) * wide + lax.div(at, piece)

    def line(i, j):
        return lax.div(i, wide) == lax.div(j, wide)

    outs = [[((g * chips + k) * piece, piece) for g in range(cores)] for k in range(chips)]
    *blocks, w, wo = sublayer(
        mine + theirs, gain, 1, LANES, line, outs, held=held, ahead=weights,
        inner=to_lines, leave=to_pieces, name="horizontal",
    )
    blocks = send(blocks)
    crossed = []
    for group in groups:
        other = jnp.concatenate([blocks[k][piece:] for k in group], 0)
        crossed.append(lax.ppermute(other, "sub", swap))

    def to_columns():
        tok, sub = lax.axis_index("tok"), lax.axis_index("sub")
        at = row_index(count)
        t, row = lax.div(at, rows), lax.rem(at, rows)
        chip, rest = lax.div(row, cores * share), lax.rem(row, cores * share)
        core, r = lax.div(rest, share), lax.rem(rest, share)
        k = chip ^ tok
        inside = t * share + r
        return jnp.where(core == sub, k * (cores * piece), chips * cores * piece + k * piece) + inside

    def column(i, j):
        return lax.div(i, rows) == lax.div(j, rows)

    (state,) = sublayer(
        blocks + crossed, gain, 2, 4 * rows, column, [[(0, count)]], held=(w, wo),
        enter=to_columns, name="vertical",
    )
    return state.reshape(video.shape)


def body(video, norm_gain, qkv_weight, out_weight):
    gain, weights = gather_weights(norm_gain, qkv_weight, out_weight)
    frames, rows, cols, _ = video.shape
    chips, cores = lax.axis_size("tok"), lax.axis_size("sub")
    piece = frames * rows // (chips * cores)
    if cols == 1 and cores == 2 and chips & (chips - 1) == 0 and rows % (chips * cores) == 0 and piece % 8 == 0 and LANES % (chips * cores) == 0:
        return by_rows(video, gain, weights)
    return general(video, gain, weights)


def solution(mesh):
    in_specs = (
        P("parts", None, ("tok", "sub"), None),
        P(),
        P(None, None, None, "sub"),
        P(None, "sub", None),
    )
    out_specs = P("parts", None, ("tok", "sub"), None)
    return jax.shard_map(body, mesh=mesh, in_specs=in_specs, out_specs=out_specs, check_vma=False)
```
